512 devices in a mesh: layer: 32 (over x_lo, y, core), feat: 16 (over z, x_hi).
Axes of the slice: x: 4 (x_hi: 2, x_lo: 2; x = x_hi * 2 + x_lo), y: 8, z: 8, core: 2. Of those that a mesh axis runs over, the one named last changes fastest.
Arguments:
- latents: bfloat16 [2048, 16384], P('layer', 'feat'), may hold values from 0.5 to 3
- block_lists: int32 [4, 16, 64], replicated, may hold values from 0 to 127, all different within a row
- decoders: bfloat16 [2, 16384, 32768], P(None, 'feat', 'layer'), may hold values from -0.03125 to 0.03125
- targets: bfloat16 [512, 32768], P('feat', 'layer'), may hold values from -6 to 6
Outputs:
- errors: bfloat16 [512, 32768], P('feat', 'layer')
- latent_grad: float32 [2048, 16384], P('layer', 'feat')
The draws below stay inside these ranges and needn't reach their ends.
Inputs may be any that keep to these rules, and one draw needn't show every extreme that they name: `block_lists`: each row names 64 different latent blocks, and every block is named by some row.
All inputs are finite; a program needn't handle non-finite values.
Results may differ from the reference program's by a relative error of at most 0.006.
Values may be sent and summed in bfloat16 or wider, within the bound.
No kernel may reach another device: no remote copies, remote signals or barrier semaphores. Data moves between devices by JAX's collectives and lax.ppermute only.
A program may use at most 64 MiB of HBM per device.

```python
import jax
import jax.numpy as jnp
from jax import lax

D = 8192
FEAT = 16384
BLOCK = 128
LAYERS = 4
SPAN = 2
TOK = 512
TROWS = 32
NBLK = 128
ACTIVE = 64
TBLK = 16


def shard_levels(key, extent, pieces, smallest, top_value):
    loudness = 1.0
    for dim, blocks in pieces:
        steps = jax.random.uniform(jax.random.fold_in(jax.random.fold_in(key, 6), dim), (blocks,), jnp.float32, smallest / len(pieces), top_value / len(pieces))
        loudness = loudness * jnp.repeat(jnp.exp(steps), extent[dim] // blocks).reshape((-1,) + (1,) * (len(extent) - 1 - dim))
    return loudness


def picks_of(key, rows, number_of, top, lift):
    ranking = jax.random.permutation(jax.random.fold_in(key, 1), number_of)
    pull = ranking
    for power in range(3):
        pull = pull * pull // number_of
    pull = pull * lift // number_of
    lots = jax.random.randint(jax.random.fold_in(key, 2), (rows, number_of), 0, 4096) + pull
    sure = jax.random.permutation(jax.random.fold_in(key, 3), rows)[jnp.arange(number_of) % rows]
    lots = jnp.where(jnp.arange(rows)[:, None] == sure[None, :], 1 << 14, lots)
    priority = lots * number_of + jnp.arange(number_of)
    return lax.top_k(priority.astype(jnp.int32), top)[1].astype(jnp.int32)


def scatter_about(own_key, extent, spread, bound, pieces=(), kind=jnp.bfloat16):
    entries = jax.random.normal(own_key, extent, jnp.float32) * spread
    if len(pieces) > 0:
        entries = shard_levels(own_key, extent, pieces, -0.22, 0.18) * entries
    return jnp.clip(entries, min=-bound, max=bound).astype(kind)


def setup_inputs(seed: int = 0) -> dict:
    key_of = jax.random.split(jax.random.key(seed), 5)
    return {
        "latents": jnp.clip(0.5 + 2.5 * jax.random.uniform(key_of[0], (LAYERS * TOK, FEAT), jnp.float32) ** shard_levels(key_of[0], (LAYERS * TOK, FEAT), ((0, 32), (1, 16)), -0.2, 0.2), 0.5, 3.0).astype(jnp.bfloat16),
        "block_lists": picks_of(key_of[1], LAYERS * TBLK, NBLK, ACTIVE, 8192).reshape((LAYERS, TBLK, ACTIVE)),
        "decoders": scatter_about(key_of[2], (SPAN, FEAT, LAYERS * D), (SPAN * FEAT) ** -0.5, 0.03125, ((1, 16), (2, 32))),
        "targets": scatter_about(key_of[3], (TOK, LAYERS * D), 1.0, 6.0, ((0, 16), (1, 32))),
    }


def build_mask(block_lists):
    blocks = jnp.arange(NBLK, dtype=jnp.int32)
    hit = jnp.any(block_lists[:, :, :, None] == blocks[None, None, None, :], axis=2)
    hit = jnp.repeat(hit, TROWS, axis=1)
    return jnp.repeat(hit, BLOCK, axis=2)


def reference(latents, block_lists, decoders, targets):
    mask = build_mask(block_lists)
    values = latents.reshape(LAYERS, TOK, FEAT)
    active = jnp.where(mask, values, jnp.zeros_like(values))
    before = jnp.concatenate([jnp.zeros_like(active[:1]), active[:-1]], axis=0)
    wanted_all = targets.reshape(TOK, LAYERS, D)

    def one_layer(items):
        layer_id, own, prior = items
        weights = lax.dynamic_slice_in_dim(decoders, layer_id * D, D, 2)
        wanted = lax.dynamic_index_in_dim(wanted_all, layer_id, 1, keepdims=False)
        recon = jnp.dot(own, weights[0], preferred_element_type=jnp.float32)
        recon = recon + jnp.dot(prior, weights[1], preferred_element_type=jnp.float32)
        error = (recon - wanted.astype(jnp.float32)).astype(jnp.bfloat16)
        part_own = jnp.dot(error, weights[0].T, preferred_element_type=jnp.float32)
        part_prior = jnp.dot(error, weights[1].T, preferred_element_type=jnp.float32)
        return error, part_own, part_prior

    layer_ids = jnp.arange(LAYERS, dtype=jnp.int32)
    errors, part_own, part_prior = lax.map(one_layer, (layer_ids, active, before))
    errors_out = jnp.transpose(errors, (1, 0, 2)).reshape(TOK, LAYERS * D)
    later = jnp.concatenate([part_prior[1:], jnp.zeros_like(part_prior[:1])], axis=0)
    latent_grad = jnp.where(mask, part_own + later, jnp.zeros_like(part_own))
    return errors_out, latent_grad.reshape(LAYERS * TOK, FEAT)
```

```python
import jax
import jax.numpy as jnp
from jax import lax
from jax.sharding import PartitionSpec as P

D = 8192
BLOCK = 128
TROWS = 32
CHUNKS = 1
CORES = 2


def swap_cores(value):
    count = lax.axis_size("layer")
    return lax.ppermute(value, "layer", [(source, source ^ 1) for source in range(count)])


def passed_along(value, steps):
    count = lax.axis_size("layer")
    first, last = (max(0, -steps), min(count, count - steps))
    return lax.ppermute(value, "layer", [(source, source + steps) for source in range(first, last)])


def chip_groups(groups):
    count = lax.axis_size("layer")
    return [
        [start + chip * CORES + core for chip in range(groups // CORES)]
        for start in range(0, count, groups)
        for core in range(CORES)
    ]


def over_chips(value, groups):
    return lax.all_to_all(value, "layer", 0, 0, tiled=True, axis_index_groups=chip_groups(groups))


def over_feat(value):
    return lax.all_to_all(value, "feat", 0, 0, tiled=True)


def local(latents, block_lists, decoders, targets):
    layer_pos = lax.axis_index("layer")
    feat_pos = lax.axis_index("feat")
    feats = lax.axis_size("feat")
    width_cols = decoders.shape[2]
    groups = D // width_cols
    chips = groups // CORES
    layer_id = layer_pos // groups
    member = layer_pos % groups
    upper_core = member % CORES == 1
    rows_here, feat_cols = latents.shape
    blocks_here = feat_cols // BLOCK
    lists_here = rows_here // TROWS
    sub = TROWS // CHUNKS
    piece_rows = lists_here * sub
    chunk_rows = piece_rows * groups

    lists = lax.dynamic_slice(
        block_lists,
        (layer_id, member * lists_here, 0),
        (1, lists_here, block_lists.shape[2]),
    )[0]
    wanted = feat_pos * blocks_here + jnp.arange(blocks_here, dtype=jnp.int32)
    hit = jnp.any(lists[:, :, None] == wanted[None, None, :], axis=1)
    tile_mask = jnp.repeat(jnp.repeat(hit, TROWS, axis=0), BLOCK, axis=1)
    own_tile = jnp.where(tile_mask, latents, jnp.zeros_like(latents))
    prior_tile = passed_along(own_tile, groups)

    def rows_of(value, chunk):
        split = value.reshape(-1, CHUNKS, sub, value.shape[1])
        return split[:, chunk].reshape(-1, value.shape[1])

    errors, grads = [], []
    for chunk in range(CHUNKS):
        pieces = jnp.stack([rows_of(own_tile, chunk), rows_of(prior_tile, chunk)])
        mine = over_chips(jnp.broadcast_to(pieces[None], (chips,) + pieces.shape), groups)
        theirs = swap_cores(mine)
        acts = jnp.stack(
            [jnp.where(upper_core, theirs, mine), jnp.where(upper_core, mine, theirs)], 1
        )
        acts = [acts[:, :, k].reshape(chunk_rows, feat_cols) for k in range(2)]
        summed = jnp.dot(acts[0], decoders[0], preferred_element_type=jnp.float32)
        summed = summed + jnp.dot(acts[1], decoders[1], preferred_element_type=jnp.float32)
        parts = over_feat(summed.astype(jnp.bfloat16).reshape(feats, lists_here * groups * sub // feats, width_cols))
        recon = jnp.sum(parts.astype(jnp.float32), axis=0)
        error = (recon - rows_of(targets, chunk).astype(jnp.float32)).astype(jnp.bfloat16)
        errors.append(error)
        spread = over_feat(jnp.broadcast_to(error[None], (feats,) + error.shape))
        terms = jnp.einsum(
            "tc,kfc->ktf",
            spread.reshape(chunk_rows, width_cols),
            decoders,
            preferred_element_type=jnp.float32,
        )
        terms = terms.reshape(2, chips, CORES, piece_rows, feat_cols)
        kept = jnp.where(upper_core, terms[:, :, 1], terms[:, :, 0])
        sent = jnp.where(upper_core, terms[:, :, 0], terms[:, :, 1]).astype(jnp.bfloat16)
        pair = kept + swap_cores(sent).astype(jnp.float32)
        pair = jnp.transpose(pair.astype(jnp.bfloat16), (1, 0, 2, 3))
        total = jnp.sum(over_chips(pair, groups).astype(jnp.float32), axis=0)
        from_next = passed_along(total[1].astype(jnp.bfloat16), -groups)
        grads.append(total[0] + from_next.astype(jnp.float32))

    def joined(values):
        split = [value.reshape(-1, sub, value.shape[1]) for value in values]
        return jnp.stack(split, 1).reshape(-1, values[0].shape[1])

    combined = joined(grads)
    latent_grad = jnp.where(tile_mask, combined, jnp.zeros_like(combined))
    return (joined(errors), latent_grad)


def solution(mesh):
    placed = (P("layer", "feat"), P(), P(None, "feat", "layer"), P("feat", "layer"))
    return jax.shard_map(
        local,
        mesh=mesh,
        in_specs=placed,
        out_specs=(P("feat", "layer"), P("layer", "feat")),
        check_vma=False,
    )
```

```python
import jax
import jax.numpy as jnp
from jax import lax
from jax.sharding import PartitionSpec as P


D = 8192
BLOCK = 128
TROWS = 32
CORES = 2


def swap_cores(value):
    count = lax.axis_size("layer")
    return lax.ppermute(value, "layer", [(source, source ^ 1) for source in range(count)])


def mirrored(value, groups, steps):
    count = lax.axis_size("layer")
    chips = groups // CORES
    pairs = []
    for source in range(count):
        start = source // groups * groups + steps
        chip, core = source % groups // CORES, source % CORES
        if 0 <= start < count:
            pairs.append((source, start + (chips - 1 - chip) * CORES + core))
    return lax.ppermute(value, "layer", pairs)


def to_chip(value, turn):
    count = lax.axis_size("layer")
    return lax.ppermute(
        value, "layer", [(source, source ^ (turn * CORES)) for source in range(count)]
    )


def ordered(upper, held, partner, axis):
    return jnp.stack(
        [jnp.where(upper, partner, held), jnp.where(upper, held, partner)], axis
    )


def halves(upper, value, axis):
    lower = lax.index_in_dim(value, 0, axis, keepdims=False)
    higher = lax.index_in_dim(value, 1, axis, keepdims=False)
    return jnp.where(upper, higher, lower), jnp.where(upper, lower, higher)


def over_feat(value):
    return lax.all_to_all(value, "feat", 0, 0, tiled=True)


def local(latents, block_lists, decoders, targets):
    layer_pos = lax.axis_index("layer")
    feat_pos = lax.axis_index("feat")
    feats = lax.axis_size("feat")
    width_cols = decoders.shape[2]
    groups = D // width_cols
    chips = groups // CORES
    layer_id = layer_pos // groups
    member = layer_pos % groups
    upper_core = member % CORES == 1
    upper_chip = member // CORES % 2 == 1
    upper_pair = member // (2 * CORES) % 2 == 1
    rows_here, feat_cols = latents.shape
    total_rows = rows_here * groups
    blocks_here = feat_cols // BLOCK
    lists_here = rows_here // TROWS

    lists = lax.dynamic_slice(
        block_lists,
        (layer_id, member * lists_here, 0),
        (1, lists_here, block_lists.shape[2]),
    )[0]
    wanted = feat_pos * blocks_here + jnp.arange(blocks_here, dtype=jnp.int32)
    hit = jnp.any(lists[:, :, None] == wanted[None, None, :], axis=1)
    tile_mask = jnp.repeat(jnp.repeat(hit, TROWS, axis=0), BLOCK, axis=1)
    own_tile = jnp.where(tile_mask, latents, jnp.zeros_like(latents))
    prior_tile = mirrored(own_tile, groups, groups)

    def spread_over_chips(piece, high, low):
        far = to_chip(piece, 2)
        pair = ordered(high, piece, far, 0)
        near = to_chip(pair, 1)
        return ordered(low, pair, near, 1).reshape(chips, rows_here, feat_cols)

    own_mine = spread_over_chips(own_tile, upper_pair, upper_chip)
    prior_mine = spread_over_chips(
        prior_tile, jnp.logical_not(upper_pair), jnp.logical_not(upper_chip)
    )
    own_theirs = swap_cores(own_mine)
    prior_theirs = swap_cores(prior_mine)
    acts_own = ordered(upper_core, own_mine, own_theirs, 1)
    own_part = jnp.dot(
        acts_own.reshape(total_rows, feat_cols),
        decoders[0],
        preferred_element_type=jnp.float32,
    )
    acts_prior = ordered(lax.optimization_barrier(upper_core), prior_mine, prior_theirs, 1)
    prior_part = jnp.dot(
        acts_prior.reshape(total_rows, feat_cols),
        decoders[1],
        preferred_element_type=jnp.float32,
    )
    summed = prior_part + own_part
    parts = over_feat(summed.astype(jnp.bfloat16).reshape(feats, -1, width_cols))
    recon = jnp.sum(parts.astype(jnp.float32), axis=0)
    errors = (recon - targets.astype(jnp.float32)).astype(jnp.bfloat16)
    spread = over_feat(jnp.broadcast_to(errors[None], (feats,) + errors.shape))
    spread = spread.reshape(total_rows, width_cols)

    def paired(weights):
        terms = jnp.einsum("tc,fc->tf", spread, weights, preferred_element_type=jnp.float32)
        terms = terms.reshape(chips, CORES, rows_here, feat_cols)
        kept, sent = halves(upper_core, terms, 1)
        return kept + swap_cores(sent.astype(jnp.bfloat16)).astype(jnp.float32)

    def summed_over_chips(total, high, low):
        total = total.reshape(2, chips // 2, rows_here, feat_cols)
        kept, sent = halves(low, total, 1)
        near = to_chip(sent.astype(jnp.bfloat16), 1)
        total = kept + near.astype(jnp.float32)
        kept, sent = halves(high, total, 0)
        far = to_chip(sent.astype(jnp.bfloat16), 2)
        return kept + far.astype(jnp.float32)

    to_prior = summed_over_chips(
        paired(decoders[1]), jnp.logical_not(upper_pair), jnp.logical_not(upper_chip)
    )
    from_next = mirrored(to_prior.astype(jnp.bfloat16), groups, -groups)
    from_next = from_next.astype(jnp.float32)
    combined = summed_over_chips(paired(decoders[0]), upper_pair, upper_chip) + from_next
    latent_grad = jnp.where(tile_mask, combined, jnp.zeros_like(combined))
    return (errors, latent_grad)


def solution(mesh):
    placed = (P("layer", "feat"), P(), P(None, "feat", "layer"), P("feat", "layer"))
    return jax.shard_map(
        local,
        mesh=mesh,
        in_specs=placed,
        out_specs=(P("feat", "layer"), P("layer", "feat")),
        check_vma=False,
    )
```

```python
import jax
import jax.numpy as jnp
from jax import lax
from jax.sharding import PartitionSpec as P


D = 8192
BLOCK = 128
TROWS = 32
CORES = 2


def swap_cores(value):
    count = lax.axis_size("layer")
    return lax.ppermute(value, "layer", [(source, source ^ 1) for source in range(count)])


def mirrored(value, groups, steps, turn=0):
    count = lax.axis_size("layer")
    chips = groups // CORES
    pairs = []
    for source in range(count):
        start = source // groups * groups + steps
        chip, core = source % groups // CORES, source % CORES
        if 0 <= start < count:
            pairs.append((source, start + (chips - 1 - chip ^ turn) * CORES + core))
    return lax.ppermute(value, "layer", pairs)


def to_chip(value, turn):
    count = lax.axis_size("layer")
    return lax.ppermute(
        value, "layer", [(source, source ^ (turn * CORES)) for source in range(count)]
    )


def ordered(upper, held, partner, axis):
    return jnp.stack(
        [jnp.where(upper, partner, held), jnp.where(upper, held, partner)], axis
    )


def halves(upper, value, axis):
    lower = lax.index_in_dim(value, 0, axis, keepdims=False)
    higher = lax.index_in_dim(value, 1, axis, keepdims=False)
    return jnp.where(upper, higher, lower), jnp.where(upper, lower, higher)


def over_feat(value):
    return lax.all_to_all(value, "feat", 0, 0, tiled=True)


def local(latents, block_lists, decoders, targets):
    layer_pos = lax.axis_index("layer")
    feat_pos = lax.axis_index("feat")
    feats = lax.axis_size("feat")
    width_cols = decoders.shape[2]
    groups = D // width_cols
    chips = groups // CORES
    layer_id = layer_pos // groups
    member = layer_pos % groups
    upper_core = member % CORES == 1
    upper_chip = member // CORES % 2 == 1
    upper_pair = member // (2 * CORES) % 2 == 1
    rows_here, feat_cols = latents.shape
    total_rows = rows_here * groups
    blocks_here = feat_cols // BLOCK
    lists_here = rows_here // TROWS

    lists = lax.dynamic_slice(
        block_lists,
        (layer_id, member * lists_here, 0),
        (1, lists_here, block_lists.shape[2]),
    )[0]
    wanted = feat_pos * blocks_here + jnp.arange(blocks_here, dtype=jnp.int32)
    hit = jnp.any(lists[:, :, None] == wanted[None, None, :], axis=1)
    tile_mask = jnp.repeat(jnp.repeat(hit, TROWS, axis=0), BLOCK, axis=1)
    own_tile = jnp.where(tile_mask, latents, jnp.zeros_like(latents))
    prior_tile = mirrored(own_tile, groups, groups)
    prior_far = mirrored(own_tile, groups, groups, 2)

    def spread_over_chips(piece, far, high, low):
        pair = ordered(high, piece, far, 0)
        near = to_chip(pair, 1)
        return ordered(low, pair, near, 1).reshape(chips, rows_here, feat_cols)

    own_far = to_chip(own_tile, 2)
    own_mine = spread_over_chips(own_tile, own_far, upper_pair, upper_chip)
    prior_mine = spread_over_chips(
        prior_tile, prior_far, jnp.logical_not(upper_pair), jnp.logical_not(upper_chip)
    )
    own_theirs = swap_cores(own_mine)
    prior_theirs = swap_cores(prior_mine)
    acts_own = ordered(upper_core, own_mine, own_theirs, 1)
    own_part = jnp.dot(
        acts_own.reshape(total_rows, feat_cols),
        decoders[0],
        preferred_element_type=jnp.float32,
    )
    acts_prior = ordered(lax.optimization_barrier(upper_core), prior_mine, prior_theirs, 1)
    prior_part = jnp.dot(
        acts_prior.reshape(total_rows, feat_cols),
        decoders[1],
        preferred_element_type=jnp.float32,
    )
    summed = prior_part + own_part
    parts = over_feat(summed.astype(jnp.bfloat16).reshape(feats, -1, width_cols))
    recon = jnp.sum(parts.astype(jnp.float32), axis=0)
    errors = (recon - targets.astype(jnp.float32)).astype(jnp.bfloat16)
    spread = over_feat(jnp.broadcast_to(errors[None], (feats,) + errors.shape))
    spread = spread.reshape(total_rows, width_cols)

    def paired(weights):
        terms = jnp.einsum("tc,fc->tf", spread, weights, preferred_element_type=jnp.float32)
        terms = terms.reshape(chips, CORES, rows_here, feat_cols)
        kept, sent = halves(upper_core, terms, 1)
        return kept + swap_cores(sent.astype(jnp.bfloat16)).astype(jnp.float32)

    def near_summed(total, low):
        total = total.reshape(2, chips // 2, rows_here, feat_cols)
        kept, sent = halves(low, total, 1)
        near = to_chip(sent.astype(jnp.bfloat16), 1)
        return kept + near.astype(jnp.float32)

    to_prior = near_summed(paired(decoders[1]), jnp.logical_not(upper_chip))
    to_prior = halves(jnp.logical_not(upper_pair), to_prior.astype(jnp.bfloat16), 0)
    from_next = [mirrored(to_prior[0], groups, -groups), mirrored(to_prior[1], groups, -groups, 2)]
    kept, sent = halves(upper_pair, near_summed(paired(decoders[0]), upper_chip), 0)
    far = to_chip(sent.astype(jnp.bfloat16), 2)
    combined = kept + far.astype(jnp.float32)
    combined = combined + from_next[0].astype(jnp.float32) + from_next[1].astype(jnp.float32)
    latent_grad = jnp.where(tile_mask, combined, jnp.zeros_like(combined))
    return (errors, latent_grad)


def solution(mesh):
    placed = (P("layer", "feat"), P(), P(None, "feat", "layer"), P("feat", "layer"))
    return jax.shard_map(
        local,
        mesh=mesh,
        in_specs=placed,
        out_specs=(P("feat", "layer"), P("layer", "feat")),
        check_vma=False,
    )
```
